32 devices in a mesh: groups: 2 (over y), ctx: 16 (over z, x, core).
Axes of the slice: x: 2, y: 2, z: 4, core: 2. Of those that a mesh axis runs over, the one named last changes fastest.
Arguments:
- inputs: bfloat16 [8192, 1024], P(('groups', 'ctx')), parts along dimension 0, may hold values from -6 to 6
- raw_steps: bfloat16 [8192, 32], P(('groups', 'ctx')), parts along dimension 0, may hold values from -3.2 to 3.2
- in_maps: bfloat16 [8192, 256], P(('groups', 'ctx')), parts along dimension 0, may hold values from -6 to 6
- out_maps: bfloat16 [8192, 256], P(('groups', 'ctx')), parts along dimension 0, may hold values from -0.01171875 to 0.01171875
- cotangent: bfloat16 [8192, 1024], P(('groups', 'ctx')), parts along dimension 0, may hold values from -6 to 6
- complement: int32 [512], replicated, may hold values from 0 to 511, as said below
- log_rates: float32 [16], replicated, as said below
- step_bias: float32 [16], replicated, may hold values from -0.5 to 0.5
- skip_gain: float32 [16], replicated, may hold values from 0.5 to 1.5
Outputs:
- mixed: bfloat16 [8192, 1024], P(('groups', 'ctx')), parts along dimension 0
- grad_inputs: bfloat16 [8192, 1024], P(('groups', 'ctx')), parts along dimension 0
- grad_heads: float32 [6, 16], P('groups'), parts along dimension 0
The draws below stay inside these ranges and needn't reach their ends.
There are 2 independent parts, one for each index of `groups`. The reference program is written for one: setup_inputs(seed, part) draws one part's arguments, and reference() takes and returns one part's arrays. A program takes and returns all parts, laid end to end along the dimension named above; an argument that names none is the same for every part. Nothing has to cross between parts.
Inputs may be any that keep to these rules, and one draw needn't show every extreme that they name: complement is an involution without fixed points: complement[complement[c]] = c and complement[c] != c. Each head's exp(log_rates) lies between 1 / 4096 and 0.05.
All inputs are finite; a program needn't handle non-finite values.
Results may differ from the reference program's by a relative error of at most 0.001.
Values sent between devices are 32-bit elements; how exact they have to be, the bound alone decides.
A program may use at most 256 MiB of HBM per device.

```python
import jax
import jax.numpy as jnp
from jax import lax

HEADS = 16
HEAD_DIM = 32
STATE = 128
BLOCK = 128
TOK_DEV = 256
TOKENS = 4096


def draw_raw_steps(key, part):
    noise_key, offset_key = jax.random.split(jax.random.fold_in(key, 11))
    block_total = TOKENS // TOK_DEV
    noise = jnp.clip(0.5 * jax.random.normal(noise_key, (TOKENS, 2 * HEADS), jnp.float32), -2.0, 2.0)
    offset = jax.random.uniform(offset_key, (block_total, 1, 2 * HEADS), jnp.float32, -1.2, 1.2)
    shifted = noise.reshape(block_total, TOK_DEV, 2 * HEADS) + offset
    return shifted.reshape(TOKENS, 2 * HEADS).astype(jnp.bfloat16)


def draw_log_rates(key, part):
    pick_key, fast_key, slow_key = jax.random.split(jax.random.fold_in(key, 23), 3)
    share = 5
    fast = jax.random.randint(pick_key, (HEADS,), 0, 10) < share
    fast_rate = jax.random.uniform(fast_key, (HEADS,), jnp.float32, 0.03, 0.05)
    slow_rate = jnp.exp(jax.random.uniform(slow_key, (HEADS,), jnp.float32, 0.0, 1.6094)) / TOKENS
    return jnp.log(jnp.where(fast, fast_rate, slow_rate)).astype(jnp.float32)


def draw_complement(key, part):
    order = jax.random.permutation(jax.random.fold_in(key, 37), HEADS * HEAD_DIM).astype(jnp.int32)
    partner = order.reshape(-1, 2)[:, ::-1].reshape(-1)
    return jnp.zeros((HEADS * HEAD_DIM,), jnp.int32).at[order].set(partner)


def steps_of(stream_key, extent, shards, low, top_value):
    level, own = 1.0, jax.random.fold_in(stream_key, 6)
    for dim, blocks in shards:
        steps = jnp.exp(jax.random.uniform(jax.random.fold_in(own, dim), (blocks,), jnp.float32, low / len(shards), top_value / len(shards)))
        level = level * jnp.repeat(steps, extent[dim] // blocks).reshape([-1 if axis == dim else 1 for axis in range(len(extent))])
    return level


def scatter_about(rng, shape, deviation, limit, shards=(), held_as=jnp.bfloat16):
    values = jax.random.normal(rng, shape, jnp.float32) * deviation
    if len(shards) > 0:
        values = steps_of(rng, shape, shards, -0.22, 0.18) * values
    return jnp.clip(values, min=-limit, max=limit).astype(held_as)


def setup_inputs(seed: int = 0, part: int = 0) -> dict:
    splits = jax.random.split(jax.random.key(seed), 10)
    part_keys = jax.random.split(jax.random.fold_in(splits[9], part), 10)
    inputs = scatter_about(part_keys[0], (TOKENS, 2 * HEADS * HEAD_DIM), 1.0, 6.0, ((0, 16),))
    raw_steps = draw_raw_steps(jax.random.fold_in(jax.random.fold_in(splits[9], part), 71), part)
    in_maps = scatter_about(part_keys[2], (TOKENS, 2 * STATE), 1.0, 6.0, ((0, 16),))
    out_maps = scatter_about(part_keys[3], (TOKENS, 2 * STATE), (STATE * TOKENS // 2) ** -0.5, 0.01171875, ((0, 16),))
    cotangent = scatter_about(part_keys[4], (TOKENS, 2 * HEADS * HEAD_DIM), 1.0, 6.0, ((0, 16),))
    complement = draw_complement(jax.random.fold_in(splits[9], 71), part)
    log_rates = draw_log_rates(jax.random.fold_in(splits[9], 71), part)
    step_bias = jnp.clip(jax.random.uniform(splits[7], (HEADS,), jnp.float32, -0.5, 0.5), -0.5, 0.5)
    skip_gain = jnp.clip(jax.random.uniform(splits[8], (HEADS,), jnp.float32, 0.5, 1.5), 0.5, 1.5)
    return dict(inputs=inputs, raw_steps=raw_steps, in_maps=in_maps, out_maps=out_maps, cotangent=cotangent, complement=complement, log_rates=log_rates, step_bias=step_bias, skip_gain=skip_gain)


masked_log = -1e+30
highest = lax.Precision.HIGHEST

def block_pass(state, block, decay_rate, skip_gain):
    values, step_sizes, in_map, out_map = block
    length = values.shape[0]
    log_decay = jnp.cumsum(step_sizes * decay_rate[None, :], axis=0)
    head_log = log_decay.T
    positions = jnp.arange(length)
    causal = (positions[:, None] >= positions[None, :])[None, :, :]
    spread = jnp.where(causal, head_log[:, :, None] - head_log[:, None, :], masked_log)
    affinity = jnp.dot(out_map, in_map.T, precision=highest)
    mixing = jnp.exp(spread) * affinity[None, :, :] * step_sizes.T[:, None, :]
    within = jnp.einsum('hts,shp->thp', mixing, values, precision=highest)
    entering = jnp.einsum('tn,hpn->thp', out_map, state, precision=highest)
    output = within + entering * jnp.exp(log_decay)[:, :, None] + skip_gain[None, :, None] * values
    to_end = jnp.exp(log_decay[-1][None, :] - log_decay) * step_sizes
    update = jnp.einsum('tn,thp->hpn', in_map, to_end[:, :, None] * values, precision=highest)
    state = jnp.exp(log_decay[-1])[:, None, None] * state + update
    return (state, output)

def strand_block(values, raw_steps, in_map, out_map, log_rates, step_bias, skip_gain):
    row_count, channels = values.shape
    head_count = log_rates.shape[0]
    head_depth = channels // head_count
    state_size = in_map.shape[1]
    block_count = row_count // BLOCK
    step_sizes = jax.nn.softplus(raw_steps.astype(jnp.float32) + step_bias[None, :])
    decay_rate = -jnp.exp(log_rates)
    blocks = (values.reshape(block_count, BLOCK, head_count, head_depth), step_sizes.reshape(block_count, BLOCK, head_count), in_map.astype(jnp.float32).reshape(block_count, BLOCK, state_size), out_map.astype(jnp.float32).reshape(block_count, BLOCK, state_size))
    zero_state = jnp.zeros((head_count, head_depth, state_size), jnp.float32)
    step_call = jax.checkpoint(lambda carry, block: block_pass(carry, block, decay_rate, skip_gain))
    last_state, outputs = lax.scan(step_call, zero_state, blocks)
    return outputs.reshape(row_count, channels)

def strand_layer(values, raw_steps, in_maps, out_maps, complement, log_rates, step_bias, skip_gain):
    channels = HEADS * HEAD_DIM
    near = strand_block(values[:, :channels], raw_steps[:, :HEADS], in_maps[:, :STATE], out_maps[:, :STATE], log_rates, step_bias, skip_gain)
    far_in = jnp.flip(values[:, channels:][:, complement], 0)
    far = strand_block(far_in, jnp.flip(raw_steps[:, HEADS:], 0), jnp.flip(in_maps[:, STATE:], 0), jnp.flip(out_maps[:, STATE:], 0), log_rates, step_bias, skip_gain)
    return jnp.concatenate([near, jnp.flip(far, 0)[:, complement]], axis=1)

def reference(inputs, raw_steps, in_maps, out_maps, cotangent, complement, log_rates, step_bias, skip_gain):

    def layer_call(values, rates, biases, gains):
        return strand_layer(values, raw_steps, in_maps, out_maps, complement, rates, biases, gains)
    result, pullback = jax.vjp(layer_call, inputs.astype(jnp.float32), log_rates, step_bias, skip_gain)
    grad_values, grad_rates, grad_biases, grad_gains = pullback(cotangent.astype(jnp.float32))
    scale = 1.0 / jnp.sqrt(jnp.float32(TOKENS * HEAD_DIM))
    grad_heads = jnp.stack([grad_rates, grad_biases, grad_gains]) * scale
    return (result.astype(jnp.bfloat16), grad_values.astype(jnp.bfloat16), grad_heads)
```

```python
import functools
import math

import jax
import jax.numpy as jnp
from jax import lax
from jax.experimental import pallas as pl
from jax.experimental.pallas import tpu as pltpu
from jax.sharding import PartitionSpec as P

MESH = pl.DeviceIdType.MESH
f32 = jnp.float32
bf16 = jnp.bfloat16
NN = (((1,), (0,)), ((), ()))
NT = (((1,), (1,)), ((), ()))
TN = (((0,), (0,)), ((), ()))
PIECES = 4


def mm(a, b, dims):
    return lax.dot_general(a, b, dims, preferred_element_type=f32)


def split(x):
    high = x.astype(bf16)
    return high, (x - high.astype(f32)).astype(bf16)


def mm_exact(x, b, dims):
    first = x.astype(bf16)
    rest = x - first.astype(f32)
    second = rest.astype(bf16)
    third = (rest - second.astype(f32)).astype(bf16)
    return mm(first, b, dims) + (mm(second, b, dims) + mm(third, b, dims))


def indicator(condition):
    return jnp.where(condition, 1.0, 0.0).astype(bf16)


def widen(x, depth, lanes=None):
    lanes = x.shape[1] if lanes is None else lanes
    return jnp.concatenate(
        [jnp.broadcast_to(x[h : h + 1, :], (depth, lanes)) for h in range(x.shape[0])], axis=0
    )


def narrow(x, depth):
    return jnp.concatenate(
        [
            jnp.sum(x[h * depth : (h + 1) * depth, :], axis=0, keepdims=True)
            for h in range(x.shape[0] // depth)
        ],
        axis=0,
    )


def column(row):
    size = row.shape[1]
    eye = lax.broadcasted_iota(jnp.int32, (size, size), 0) == lax.broadcasted_iota(
        jnp.int32, (size, size), 1
    )
    return jnp.sum(jnp.where(eye, row, 0.0), axis=1, keepdims=True)


def layer_kernel(
    n,
    scale,
    x_hbm,
    r_hbm,
    b_hbm,
    c_hbm,
    g_hbm,
    comp_hbm,
    rates_hbm,
    bias_hbm,
    gain_hbm,
    mixed_ref,
    grad_ref,
    heads_ref,
    x_ref,
    r_ref,
    b_ref,
    c_ref,
    g_ref,
    comp_ref,
    rates_ref,
    bias_ref,
    gain_ref,
    load_sem,
    perm,
    out_all,
    v_all,
    g_all,
    u_all,
    w_all,
    y_all,
    dv_all,
    local,
    entry,
    pair_in,
    pair_sum,
    quad_in,
    quad_sum,
    chain_in,
    chain_out,
    chip_out,
    chip_in,
    core_out,
    shares,
    sums,
    share_send,
    share_recv,
    send_sem,
    recv_sem,
    sums_send,
    sums_recv,
):
    me = lax.axis_index("ctx")
    rows, width = x_hbm.shape[0], x_hbm.shape[1] // 2
    heads = rates_hbm.shape[1]
    depth = width // heads
    states = b_hbm.shape[1] // 2
    quarter = width // 2
    piece = quarter // PIECES
    piece_heads = piece // depth
    quads = n // 4
    quad, seat = me // 4, lax.rem(me, 4)
    chip, core = seat // 2, lax.rem(seat, 2)

    loads = [
        pltpu.make_async_copy(source, target, load_sem.at[i])
        for i, (source, target) in enumerate(
            (
                (r_hbm, r_ref),
                (rates_hbm, rates_ref),
                (bias_hbm, bias_ref),
                (gain_hbm, gain_ref),
                (comp_hbm, comp_ref),
                (x_hbm, x_ref),
                (g_hbm, g_ref),
                (b_hbm, b_ref),
                (c_hbm, c_ref),
            )
        )
    ]
    for load in loads:
        load.start()
    barrier = pltpu.get_barrier_semaphore()

    def greet(i, carry):
        pl.semaphore_signal(
            barrier, inc=1, device_id={"ctx": lax.rem(me + i, n)}, device_id_type=MESH
        )
        return carry

    lax.fori_loop(1, n, greet, 0)

    chan_row = lax.broadcasted_iota(jnp.int32, (width, width), 0)
    chan_col = lax.broadcasted_iota(jnp.int32, (width, width), 1)
    perm[0] = indicator(chan_row == chan_col)

    at_row = lax.broadcasted_iota(jnp.int32, (rows, rows), 0)
    at_col = lax.broadcasted_iota(jnp.int32, (rows, rows), 1)
    masks = (at_col <= at_row, at_col >= at_row)

    for load in loads[:5]:
        load.wait()
    perm[1] = indicator(chan_row == jnp.broadcast_to(comp_ref[...], (width, width)))
    rate = -jnp.exp(column(rates_ref[...]))
    bias = column(bias_ref[...])
    gain = column(gain_ref[...])
    gain_rows = widen(jnp.broadcast_to(gain, (heads, rows)), depth)
    raw = r_ref[...].astype(f32)

    prepared = []
    for k in range(2):
        logits = raw[k * heads : (k + 1) * heads, :] + bias
        small = jnp.exp(-jnp.abs(logits))
        steps = jnp.maximum(logits, 0.0) + jnp.log(1.0 + small)
        slope = 1.0 / (1.0 + jnp.exp(-logits))
        reach = indicator(masks[k])
        log_decay = mm_exact(steps, reach, NT) * rate
        total = log_decay[:, rows - 1 : rows] if k == 0 else log_decay[:, 0:1]
        half = 0.5 * total
        shares[seat, k * heads : (k + 1) * heads] = jnp.broadcast_to(
            jnp.exp(total), (heads, states)
        )
        prepared.append((steps, slope, reach, log_decay, half))

    pl.semaphore_wait(barrier, n - 1)

    def share(i, theirs):
        at = lax.rem(seat + i, 4) if theirs else seat
        to = quad * 4 + lax.rem(seat + i, 4)
        return pltpu.make_async_remote_copy(
            src_ref=shares.at[at],
            dst_ref=shares.at[at],
            send_sem=share_send.at[i],
            recv_sem=share_recv.at[at],
            device_id={"ctx": to},
            device_id_type=MESH,
        )

    for i in range(1, 4):
        share(i, False).start()

    for load in loads[5:]:
        load.wait()

    kept = []
    for k in range(2):
        steps, slope, reach, log_decay, half = prepared[k]
        u_all[k] = widen(jnp.exp(log_decay - half), depth)
        w_all[k] = widen(steps * jnp.exp(half - log_decay), depth)
        half_rows = widen(jnp.broadcast_to(jnp.exp(half), (heads, states)), depth)
        v_rows = mm(perm[k], x_ref[:, k * width : (k + 1) * width], NT)
        g_rows = mm(perm[k], g_ref[:, k * width : (k + 1) * width], NT)
        v_all[k] = v_rows.astype(bf16)
        g_all[k] = g_rows.astype(bf16)
        v_high, v_low = split(v_rows * w_all[k])
        g_high, g_low = split(g_rows * u_all[k])
        b_here = b_ref[:, k * states : (k + 1) * states]
        c_here = c_ref[:, k * states : (k + 1) * states]
        local[k, 0:width] = (mm(v_high, b_here, NN) + mm(v_low, b_here, NN)) * half_rows
        local[1 - k, width:] = (mm(g_high, c_here, NN) + mm(g_low, c_here, NN)) * half_rows
        kept.append((steps, slope, reach, half_rows, v_high, v_low, g_high, g_low))

    twin = quad * 4 + chip * 2 + (1 - core)
    across = quad * 4 + (1 - chip) * 2 + core

    def place(c, x, p):
        return pl.ds(pl.multiple_of(c * width + x * quarter + p * piece, piece), piece)

    def link(stage, source, target, way, at, p, to):
        return pltpu.make_async_remote_copy(
            src_ref=source.at[way, at],
            dst_ref=target.at[way, at],
            send_sem=send_sem.at[stage, way, p],
            recv_sem=recv_sem.at[stage, way, p],
            device_id={"ctx": to},
            device_id_type=MESH,
        )

    def to_twin(kind, way, p):
        x = 1 - chip if kind == 0 else chip
        return link(kind, local, pair_in, way, place(1 - core, x, p), p, twin)

    def from_twin(kind, way, p):
        x = 1 - chip if kind == 0 else chip
        return link(kind, local, pair_in, way, place(core, x, p), p, twin)

    def sum_across(way, p, x):
        return link(2, pair_sum, quad_in, way, place(core, x, p), p, across)

    def along(way, p):
        to = jnp.where(way == 0, jnp.minimum(quad + 1, quads - 1), jnp.maximum(quad - 1, 0))
        return link(3, chain_out, chain_in, way, place(core, chip, p), p, to * 4 + seat)

    def entry_across(way, p, x):
        return link(4, chip_out, chip_in, way, place(core, x, p), p, across)

    def entry_twin(kind, way, p, c):
        x = chip if kind == 0 else 1 - chip
        return link(5 + kind, core_out, entry, way, place(c, x, p), p, twin)

    def share_rows(who, way, x, p):
        strand = way + core - 2 * way * core
        first = strand * heads + x * (heads // 2) + p * piece_heads
        return jnp.concatenate(
            [
                jnp.broadcast_to(shares[who, pl.ds(first + i, 1), :], (depth, states))
                for i in range(piece_heads)
            ],
            axis=0,
        )

    nearer = jnp.where(2 * quad < quads, 0, 1)

    def every(body):
        def step(s, carry):
            turn = s // PIECES
            body(turn + nearer - 2 * turn * nearer, lax.rem(s, PIECES))
            return carry

        lax.fori_loop(0, 2 * PIECES, step, 0)

    for kind in range(2):
        every(lambda way, p: to_twin(kind, way, p).start())

    for i in range(1, 4):
        share(i, True).wait_recv()

    def combine(mine, theirs, mine_first, decay):
        early = jnp.where(mine_first, mine, theirs)
        late = jnp.where(mine_first, theirs, mine)
        return decay * early + late

    def add_pair(kind, way, p):
        from_twin(kind, way, p).wait_recv()
        x = 1 - chip if kind == 0 else chip
        at = place(core, x, p)
        decay = share_rows(chip * 2 + 1 - way, way, x, p)
        pair_sum[way, at] = combine(local[way, at], pair_in[way, at], core == way, decay)
        if kind == 0:
            sum_across(way, p, x).start()

    for kind in range(2):
        every(lambda way, p: add_pair(kind, way, p))

    for k in range(2):
        steps, slope, reach, half_rows, v_high, v_low, g_high, g_low = kept[k]
        b_here = b_ref[:, k * states : (k + 1) * states]
        c_here = c_ref[:, k * states : (k + 1) * states]
        near_high, near_low = split(jnp.where(masks[k], mm(c_here, b_here, NT), 0.0))
        y_all[k] = mm(v_high, near_high, NT) + (mm(v_high, near_low, NT) + mm(v_low, near_high, NT))
        dv_all[k] = mm(g_high, near_high, NN) + (
            mm(g_high, near_low, NN) + mm(g_low, near_high, NN)
        )

    def pair_decay(x_owner, way, x, p):
        return share_rows(x_owner * 2, way, x, p) * share_rows(x_owner * 2 + 1, way, x, p)

    def add_quad(way, p):
        sum_across(way, p, chip).wait_recv()
        at = place(core, chip, p)
        decay = pair_decay(1 - way, way, chip, p)
        quad_sum[way, at] = combine(pair_sum[way, at], quad_in[way, at], chip == way, decay)
        opens = quad == way * (quads - 1)

        @pl.when(opens)
        def _():
            chain_in[way, at] = jnp.zeros((piece, states), f32)
            chain_out[way, at] = quad_sum[way, at]

        @pl.when(opens & (quads > 1))
        def _():
            along(way, p).start()

    every(add_quad)

    def hand_out(kind, way, p, pair_entry):
        x = chip if kind == 0 else 1 - chip
        at = place(core, x, p)
        early = jnp.where(core == way, local[way, at], pair_in[way, at])
        later_entry = share_rows(chip * 2 + way, way, x, p) * pair_entry + early
        core_out[way, at] = jnp.where(core == way, later_entry, pair_entry)
        entry_twin(kind, way, p, core).start()
        entry[way, at] = jnp.where(core == way, pair_entry, later_entry)

    def pass_on(way, p):
        at = place(core, chip, p)

        @pl.when(quad != way * (quads - 1))
        def _():
            along(way, p).wait_recv()

            @pl.when(quad != (1 - way) * (quads - 1))
            def _():
                decay = pair_decay(0, way, chip, p) * pair_decay(1, way, chip, p)
                chain_out[way, at] = decay * chain_in[way, at] + quad_sum[way, at]
                along(way, p).start()

        arrived = chain_in[way, at]
        early = jnp.where(chip == way, pair_sum[way, at], quad_in[way, at])
        later_entry = pair_decay(way, way, chip, p) * arrived + early
        chip_out[way, at] = jnp.where(chip == way, later_entry, arrived)
        entry_across(way, p, chip).start()
        hand_out(0, way, p, jnp.where(chip == way, arrived, later_entry))

    every(pass_on)

    def pass_down(way, p):
        entry_across(way, p, 1 - chip).wait_recv()
        hand_out(1, way, p, chip_in[way, place(core, 1 - chip, p)])

    every(pass_down)

    def arrive(way, p):
        for kind in range(2):
            entry_twin(kind, way, p, 1 - core).wait_recv()

    every(arrive)

    terms = [0.0, 0.0, 0.0]
    for k in range(2):
        steps, slope, reach, half_rows, v_high, v_low, g_high, g_low = kept[k]
        b_here = b_ref[:, k * states : (k + 1) * states]
        c_here = c_ref[:, k * states : (k + 1) * states]
        after = entry[1 - k, width:]
        s_high, s_low = split(entry[k, 0:width] * half_rows)
        a_high, a_low = split(after * half_rows)
        y = (y_all[k] + (mm(s_high, c_here, NT) + mm(s_low, c_here, NT))) * u_all[k]
        dv = (dv_all[k] + (mm(a_high, b_here, NT) + mm(a_low, b_here, NT))) * w_all[k]
        v_rows = v_all[k].astype(f32)
        g_rows = g_all[k].astype(f32)
        out = (y + gain_rows * v_rows).astype(bf16)
        dout = (dv + gain_rows * g_rows).astype(bf16)
        out_all[0, k] = out
        out_all[1, k] = dout
        back = narrow(v_rows * dv, depth)
        level = narrow(g_rows * y, depth) - back
        totals = widen(shares[seat, k * heads : (k + 1) * heads], depth)
        leaving = totals * entry[k, 0:width] + local[k, 0:width]
        edge = jnp.sum(narrow(after * leaving, depth), axis=1, keepdims=True)
        dlog = edge + mm_exact(level, reach, NN)
        terms[0] += rate * jnp.sum(steps * dlog, axis=1, keepdims=True)
        terms[1] += jnp.sum((back / steps + rate * dlog) * slope, axis=1, keepdims=True)
        terms[2] += jnp.sum(narrow(g_rows * v_rows, depth), axis=1, keepdims=True)

    lane = lax.broadcasted_iota(jnp.int32, (heads, 128), 1)
    tile = jnp.zeros((heads, 128), f32)
    for j in range(3):
        tile = jnp.where(lane == j, jnp.broadcast_to(terms[j], (heads, 128)), tile)
    sums[me] = tile

    def tell(i):
        to = lax.rem(me + i, n)
        return pltpu.make_async_remote_copy(
            src_ref=sums.at[me],
            dst_ref=sums.at[me],
            send_sem=sums_send.at[i],
            recv_sem=sums_recv.at[me],
            device_id={"ctx": to},
            device_id_type=MESH,
        )

    def hear(i):
        at = lax.rem(me + i, n)
        return pltpu.make_async_remote_copy(
            src_ref=sums.at[at],
            dst_ref=sums.at[at],
            send_sem=sums_send.at[i],
            recv_sem=sums_recv.at[at],
            device_id={"ctx": at},
            device_id_type=MESH,
        )

    def start_one(i, carry):
        tell(i).start()
        return carry

    def wait_one(i, carry):
        hear(i).wait_recv()
        return carry

    def sent_one(i, carry):
        tell(i).wait_send()
        return carry

    lax.fori_loop(1, n, start_one, 0)
    for k in range(2):
        mixed_ref[:, k * width : (k + 1) * width] = mm(out_all[0, k], perm[k], TN).astype(bf16)
        grad_ref[:, k * width : (k + 1) * width] = mm(out_all[1, k], perm[k], TN).astype(bf16)
    def all_sent(way, p):
        for kind in range(2):
            to_twin(kind, way, p).wait_send()
            entry_twin(kind, way, p, core).wait_send()
        sum_across(way, p, 1 - chip).wait_send()
        entry_across(way, p, chip).wait_send()

        @pl.when(quad != (1 - way) * (quads - 1))
        def _():
            along(way, p).wait_send()

    every(all_sent)
    for i in range(1, 4):
        share(i, False).wait_send()
    lax.fori_loop(1, n, wait_one, 0)
    summed = lax.fori_loop(0, n, lambda i, acc: acc + sums[i], jnp.zeros((heads, 128), f32))
    lax.fori_loop(1, n, sent_one, 0)
    pick_row = lax.broadcasted_iota(jnp.int32, (heads, heads), 0)
    pick_col = lax.broadcasted_iota(jnp.int32, (heads, heads), 1)
    for j in range(3):
        heads_ref[j : j + 1, :] = scale * jnp.sum(
            jnp.where(pick_row == pick_col, jnp.broadcast_to(summed[:, j : j + 1], (heads, heads)), 0.0),
            axis=0,
            keepdims=True,
        )


def store_kernel(mixed_ref, grad_ref, heads_ref, mixed_hbm, grad_hbm, heads_hbm, sem):
    stores = [
        pltpu.make_async_copy(mixed_ref, mixed_hbm, sem.at[0]),
        pltpu.make_async_copy(grad_ref, grad_hbm, sem.at[1]),
        pltpu.make_async_copy(heads_ref, heads_hbm, sem.at[2]),
    ]
    for store in stores:
        store.start()
    for store in stores:
        store.wait()


def per_device(
    inputs, raw_steps, in_maps, out_maps, cotangent, complement, log_rates, step_bias, skip_gain
):
    rows, channels = inputs.shape
    width = channels // 2
    heads = log_rates.shape[0]
    states = in_maps.shape[1] // 2
    n = lax.axis_size("ctx")
    scale = 1.0 / math.sqrt(rows * n * (width // heads))
    vmem = pl.BlockSpec(memory_space=pltpu.VMEM)
    held = pl.pallas_call(
        functools.partial(layer_kernel, n, scale),
        name="layer",
        out_shape=(
            pltpu.VMEM((rows, channels), bf16),
            pltpu.VMEM((rows, channels), bf16),
            pltpu.VMEM((3, heads), f32),
        ),
        in_specs=[pl.BlockSpec(memory_space=pltpu.HBM)] * 9,
        out_specs=(vmem,) * 3,
        scratch_shapes=[
            pltpu.VMEM((rows, channels), bf16),
            pltpu.VMEM((2 * heads, rows), bf16),
            pltpu.VMEM((rows, 2 * states), bf16),
            pltpu.VMEM((rows, 2 * states), bf16),
            pltpu.VMEM((rows, channels), bf16),
            pltpu.VMEM((1, width), jnp.int32),
            pltpu.VMEM((1, heads), f32),
            pltpu.VMEM((1, heads), f32),
            pltpu.VMEM((1, heads), f32),
            pltpu.SemaphoreType.DMA((9,)),
            pltpu.VMEM((2, width, width), bf16),
            pltpu.VMEM((2, 2, width, rows), bf16),
            pltpu.VMEM((2, width, rows), bf16),
            pltpu.VMEM((2, width, rows), bf16),
            pltpu.VMEM((2, width, rows), f32),
            pltpu.VMEM((2, width, rows), f32),
            pltpu.VMEM((2, width, rows), f32),
            pltpu.VMEM((2, width, rows), f32),
            *[pltpu.VMEM((2, 2 * width, states), f32)] * 11,
            pltpu.VMEM((4, 2 * heads, states), f32),
            pltpu.VMEM((n, heads, 128), f32),
            pltpu.SemaphoreType.DMA((4,)),
            pltpu.SemaphoreType.DMA((4,)),
            pltpu.SemaphoreType.DMA((7, 2, PIECES)),
            pltpu.SemaphoreType.DMA((7, 2, PIECES)),
            pltpu.SemaphoreType.DMA((n,)),
            pltpu.SemaphoreType.DMA((n,)),
        ],
        compiler_params=pltpu.CompilerParams(
            collective_id=0, has_side_effects=True, vmem_limit_bytes=40 * 1024 * 1024
        ),
    )(
        *[
            pltpu.with_memory_space_constraint(operand, pltpu.HBM)
            for operand in (
                inputs,
                raw_steps.T,
                in_maps,
                out_maps,
                cotangent,
                complement.reshape(1, width),
                log_rates.reshape(1, heads),
                step_bias.reshape(1, heads),
                skip_gain.reshape(1, heads),
            )
        ]
    )
    held = [pltpu.with_memory_space_constraint(h, pltpu.VMEM) for h in held]
    hbm = pl.BlockSpec(memory_space=pltpu.HBM)
    return pl.pallas_call(
        store_kernel,
        name="store",
        out_shape=(
            jax.ShapeDtypeStruct((rows, channels), bf16),
            jax.ShapeDtypeStruct((rows, channels), bf16),
            jax.ShapeDtypeStruct((3, heads), f32),
        ),
        in_specs=[vmem] * 3,
        out_specs=(hbm,) * 3,
        scratch_shapes=[pltpu.SemaphoreType.DMA((3,))],
    )(*held)


def solution(mesh):
    split_rows = P(("groups", "ctx"), None)
    in_specs = (split_rows,) * 5 + (P(),) * 4
    out_specs = (split_rows, split_rows, P("groups", None))
    return jax.shard_map(
        per_device, mesh=mesh, in_specs=in_specs, out_specs=out_specs, check_vma=False
    )
```
